1024 devices in a mesh: atom: 32 (over x, z_hi), energy: 32 (over z_lo, y, core).
Axes of the slice: x: 8, y: 8, z: 8 (z_hi: 4, z_lo: 2; z = z_hi * 2 + z_lo), core: 2. Of those that a mesh axis runs over, the one named last changes fastest.
Arguments:
- bare_green: bfloat16 [2, 12, 12, 128, 4096], P(None, None, None, 'atom', 'energy'), may hold values from -6 to 6
- coupling_grad: bfloat16 [8, 12, 12, 128], P(None, None, None, 'atom'), may hold values from -1.75 to 1.75
- neighbours: int32 [128, 8], P('atom'), may hold values from 0 to 127, as said below
- shifts: int32 [32], replicated, may hold values from 1 to 4
- strength: float32 [32], replicated, may hold values from 5e-05 to 0.0005
- occupation: float32 [32], replicated, may hold values from 0.1 to 4
Outputs:
- green: bfloat16 [2, 12, 12, 128, 4096], P(None, None, None, 'atom', 'energy')
The draws below stay inside these ranges and needn't reach their ends.
Inputs may be any that keep to these rules, and one draw needn't show every extreme that they name: Each atom's 8 neighbours differ from it by 1 to 4 in index (not necessarily distinct); in every row one lies exactly 4 away.
All inputs are finite; a program needn't handle non-finite values.
Results may differ from the reference program's by a relative error of at most 0.0071.
Values may be sent and summed in bfloat16 or wider, within the bound.
A program may use at most 32 MiB of HBM per device.

```python
import math
import jax
import jax.numpy as jnp
from jax import lax

ORB = 12
NB = 8
NW = 32
WIDTH = 4
ITERS = 1
E_DEV = 128
ATOMS = 128
ENERGIES = 4096


def draw_neighbours(key, part):
    key_one, key_two, key_three = jax.random.split(jax.random.fold_in(key, 17), 3)
    magnitudes = jax.random.randint(key_one, (ATOMS, NB), 1, WIDTH + 1)
    slot_pick = jax.random.randint(key_two, (ATOMS, 1), 0, NB)
    slot_index = jnp.arange(NB, dtype=jnp.int32)[None, :]
    magnitudes = jnp.where(slot_index == slot_pick, WIDTH, magnitudes)
    sign_pick = jnp.where(jax.random.randint(key_three, (ATOMS, NB), 0, 2) == 0, -1, 1)
    own_atom = jnp.arange(ATOMS, dtype=jnp.int32)[:, None]
    forward = own_atom + sign_pick * magnitudes
    outside = (forward < 0) | (forward >= ATOMS)
    return jnp.where(outside, own_atom - sign_pick * magnitudes, forward).astype(jnp.int32)


def draw_shifts(key, part):
    key_one, key_two, key_three = jax.random.split(jax.random.fold_in(key, 29), 3)
    values = jax.random.randint(key_one, (NW,), 1, WIDTH + 1)
    top_slot = jax.random.randint(key_two, (), 0, NW)
    low_slot = (top_slot + 1 + jax.random.randint(key_three, (), 0, NW - 1)) % NW
    slot_index = jnp.arange(NW, dtype=jnp.int32)
    values = jnp.where(slot_index == top_slot, WIDTH, values)
    return jnp.where(slot_index == low_slot, 1, values).astype(jnp.int32)


def block_levels(own_key, shape, cuts, least, largest):
    gain, own = 1.0, jax.random.fold_in(own_key, 6)
    for position, shards_of in cuts:
        steps = jnp.exp(jax.random.uniform(jax.random.fold_in(own, position), (shards_of,), jnp.float32, least / len(cuts), largest / len(cuts)))
        gain = gain * jnp.repeat(steps, shape[position] // shards_of).reshape([-1 if axis == position else 1 for axis in range(len(shape))])
    return gain


def bell_draw(rng, extent, scale, bound, cuts=(), kind=jnp.bfloat16):
    values = scale * jax.random.normal(rng, extent, jnp.float32)
    if cuts:
        values = values * block_levels(rng, extent, cuts, -0.22, 0.18)
    return jnp.clip(values, -bound, bound).astype(kind)


def setup_inputs(seed: int = 0) -> dict:
    arg_keys = jax.random.split(jax.random.key(seed), 7)
    bare_green = bell_draw(arg_keys[0], (2, ORB, ORB, ATOMS, ENERGIES), 1.0, 6.0, ((3, 32), (4, 32)))
    coupling_grad = bell_draw(arg_keys[1], (NB, ORB, ORB, ATOMS), ORB ** -0.5, 1.75, ((3, 32),))
    neighbours = draw_neighbours(jax.random.fold_in(arg_keys[6], 71), 0)
    shifts = draw_shifts(jax.random.fold_in(arg_keys[6], 71), 0)
    strength = jnp.clip(jnp.exp(jax.random.uniform(arg_keys[4], (NW,), jnp.float32, math.log(4.999999873689376e-05), math.log(0.0005))), 4.999999873689376e-05, 0.0005)
    occupation = jnp.clip(jnp.exp(jax.random.uniform(arg_keys[5], (NW,), jnp.float32, math.log(0.1), math.log(4.0))), 0.1, 4.0)
    return {"bare_green": bare_green, "coupling_grad": coupling_grad, "neighbours": neighbours, "shifts": shifts, "strength": strength, "occupation": occupation}


def coefficients(shifts, strength, occupation):
    offsets = jnp.arange(2 * WIDTH + 1, dtype=jnp.int32) - WIDTH
    lower_hit = offsets[:, None] == -shifts[None, :]
    upper_hit = offsets[:, None] == shifts[None, :]
    weights = jnp.where(lower_hit, (strength * occupation)[None, :], jnp.zeros((), jnp.float32))
    weights = weights + jnp.where(upper_hit, (strength * (occupation + 1.0))[None, :], jnp.zeros((), jnp.float32))
    return jnp.sum(weights, axis=1).astype(jnp.bfloat16)


def band_matrix(offset_weights, energy_count):
    row_index = jnp.arange(energy_count + 2 * WIDTH, dtype=jnp.int32)[:, None]
    col_index = jnp.arange(energy_count, dtype=jnp.int32)[None, :]
    gap_index = row_index - col_index - WIDTH
    offsets = jnp.arange(2 * WIDTH + 1, dtype=jnp.int32) - WIDTH
    pick_mask = gap_index[None, :, :] == offsets[:, None, None]
    table = jnp.where(pick_mask, offset_weights.astype(jnp.float32)[:, None, None], jnp.zeros((), jnp.float32))
    return jnp.sum(table, axis=0).astype(jnp.bfloat16)


def complex_product(factor_left, factor_right):
    left_real = factor_left[0].astype(jnp.float32)
    left_imag = factor_left[1].astype(jnp.float32)
    right_real = factor_right[0].astype(jnp.float32)
    right_imag = factor_right[1].astype(jnp.float32)
    real_part = jnp.einsum('ikae,kjae->ijae', left_real, right_real) - jnp.einsum('ikae,kjae->ijae', left_imag, right_imag)
    imag_part = jnp.einsum('ikae,kjae->ijae', left_real, right_imag) + jnp.einsum('ikae,kjae->ijae', left_imag, right_real)
    return jnp.stack([real_part, imag_part])


def sandwich(phonon_sum, index_row, grad_atom):
    picked = jnp.take(phonon_sum, index_row, axis=3)
    half_product = jnp.einsum('nik,rklne->rilne', grad_atom.astype(jnp.float32), picked.astype(jnp.float32)).astype(jnp.bfloat16)
    return jnp.einsum('rilne,njl->rije', half_product.astype(jnp.float32), grad_atom.astype(jnp.float32))


def energy_slab(green_now, block_index):
    start_index = (block_index * E_DEV).astype(jnp.int32)
    middle = lax.dynamic_slice_in_dim(green_now, start_index, E_DEV, 4)
    below_rim = lax.dynamic_slice_in_dim(green_now, jnp.maximum(start_index - WIDTH, 0).astype(jnp.int32), WIDTH, 4)
    above_rim = lax.dynamic_slice_in_dim(green_now, jnp.minimum(start_index + E_DEV, ENERGIES - WIDTH).astype(jnp.int32), WIDTH, 4)
    below_rim = jnp.where(block_index > 0, below_rim, jnp.zeros_like(below_rim))
    above_rim = jnp.where(block_index < ENERGIES // E_DEV - 1, above_rim, jnp.zeros_like(above_rim))
    return jnp.concatenate([below_rim, middle, above_rim], axis=4)


def reference(bare_green, coupling_grad, neighbours, shifts, strength, occupation):
    offset_weights = coefficients(shifts, strength, occupation)
    band_table = band_matrix(offset_weights, E_DEV)
    bond_grads = jnp.moveaxis(coupling_grad, 3, 0)
    green_now = bare_green
    for iteration in range(ITERS):
        def one_block(block_index, result):
            slab_values = energy_slab(green_now, block_index)
            flat_slab = slab_values.reshape(-1, E_DEV + 2 * WIDTH)
            phonon_sum = jnp.dot(flat_slab, band_table, preferred_element_type=jnp.float32).astype(jnp.bfloat16)
            phonon_sum = phonon_sum.reshape(2, ORB, ORB, ATOMS, E_DEV)

            def per_atom(atom_item):
                return sandwich(phonon_sum, atom_item[0], atom_item[1])

            self_energy = lax.map(per_atom, (neighbours, bond_grads))
            self_energy = jnp.moveaxis(self_energy, 0, 3).astype(jnp.bfloat16)
            start_index = (block_index * E_DEV).astype(jnp.int32)
            free_block = lax.dynamic_slice_in_dim(bare_green, start_index, E_DEV, 4)
            left_product = complex_product(free_block, self_energy).astype(jnp.bfloat16)
            updated_block = (free_block.astype(jnp.float32) + complex_product(left_product, free_block)).astype(jnp.bfloat16)
            return lax.dynamic_update_slice_in_dim(result, updated_block, start_index, 4)

        green_now = lax.fori_loop(0, ENERGIES // E_DEV, one_block, jnp.zeros_like(bare_green))
    return green_now
```

```python
import functools

import jax
import jax.numpy as jnp
from jax import lax
from jax.experimental import pallas as pl
from jax.experimental.pallas import tpu as pltpu
from jax.sharding import PartitionSpec as P

WIDTH = 4
MESH = pl.DeviceIdType.MESH
F32 = jnp.float32
BF16 = jnp.bfloat16


def iota(shape, dim):
    return lax.broadcasted_iota(jnp.int32, shape, dim)


def offset_weight_rows(shifts, strength, occupation):
    row = iota((8, shifts.shape[1]), 0)
    size = jnp.where(row < WIDTH, WIDTH - row, row - (WIDTH - 1))
    extra = jnp.where(row < WIDTH, 0.0, 1.0).astype(F32)
    picked = jnp.where(size == shifts, strength * (occupation + extra), 0.0)
    return jnp.sum(picked, axis=1, keepdims=True).astype(BF16).astype(F32)


def band_from_gap(gap, weights):
    table = jnp.zeros(gap.shape, F32)
    for row in range(8):
        offset = row - WIDTH if row < WIDTH else row - WIDTH + 1
        table = jnp.where(gap == offset, weights[row : row + 1, 0:1], table)
    return table


def dot(left, right):
    return jnp.dot(left, right, preferred_element_type=F32)


def kernel(
    orb, bonds, atoms, atom_count, energy_count, chunks, raw,
    x_hbm, g_hbm, nb_hbm, sh_hbm, st_hbm, oc_hbm,
    out_ref,
    xv, gv, nbs, shv, stv, ocv,
    ebuf, halo, rim, rim_in, own, left, right,
    gf, ga, mbuf, wbuf, bf, bdup, sacc, sdup, tbuf,
    load_sem, edge_send, edge_recv, rim_send, rim_recv, slab_send, slab_recv,
):
    lanes = xv.shape[-1]
    inner = orb * atoms
    per = orb // chunks
    here_a = lax.axis_index("atom")
    here_e = lax.axis_index("energy")
    sides = ((here_a + 1, here_a < atom_count - 1), (here_a - 1, here_a > 0))
    energy_sides = ((here_e - 1, here_e > 0), (here_e + 1, here_e < energy_count - 1))

    loads = [
        pltpu.make_async_copy(src, dst, load_sem.at[slot])
        for slot, (src, dst) in enumerate(
            ((x_hbm, xv), (sh_hbm, shv), (st_hbm, stv), (oc_hbm, ocv), (g_hbm, gv), (nb_hbm, nbs))
        )
    ]
    for copy in loads:
        copy.start()
    barrier = pltpu.get_barrier_semaphore()
    expected = jnp.int32(0)
    for axis, group in (("atom", sides), ("energy", energy_sides)):
        for peer, exists in group:
            expected = expected + jnp.where(exists, 1, 0)

            @pl.when(exists)
            def _():
                pl.semaphore_signal(barrier, inc=1, device_id={axis: peer}, device_id_type=MESH)

    for side, (_, exists) in enumerate(energy_sides):

        @pl.when(jnp.logical_not(exists))
        def _():
            halo[side] = jnp.zeros(halo.shape[1:], BF16)

    for landing, (_, exists) in ((right, sides[0]), (left, sides[1])):

        @pl.when(jnp.logical_not(exists))
        def _():
            landing[...] = jnp.zeros_like(landing)

    for copy in loads[1:4]:
        copy.wait()
    weights = offset_weight_rows(shv[...], stv[...], ocv[...])
    band = band_from_gap(iota((lanes, lanes), 0) - iota((lanes, lanes), 1), weights).astype(BF16)
    edge_row, edge_col = iota((8, lanes), 0), iota((8, lanes), 1)
    edge_energy = jnp.where(edge_row < WIDTH, edge_row - WIDTH, edge_row - WIDTH + lanes)
    corner = band_from_gap(edge_energy - edge_col, weights).astype(BF16)

    loads[0].wait()
    raw_count = raw * per
    flat = [
        xv[:, :raw_count].reshape(2 * raw_count * inner, lanes),
        xv[:, raw_count:].reshape(2 * (orb - raw_count) * inner, lanes),
    ]
    split = flat[0].shape[0]
    pick_row, pick_col = iota((16, lanes), 0), iota((16, lanes), 1)
    target = jnp.where(pick_row < 8, pick_row - WIDTH, pick_row - 8 + lanes - WIDTH)
    pick = jnp.where((pick_col == target) & (pick_row >= WIDTH) & (pick_row < 12), 1.0, 0.0).astype(BF16)
    edges = [
        lax.dot_general(pick, part, (((1,), (1,)), ((), ())), preferred_element_type=F32).astype(BF16)
        for part in flat
    ]
    for side in range(2):
        ebuf[side, :, :split] = edges[0][side * 8 : side * 8 + 8]
        ebuf[side, :, split:] = edges[1][side * 8 : side * 8 + 8]

    pl.semaphore_wait(barrier, expected)

    def edge_copy(side):
        return pltpu.make_async_remote_copy(
            src_ref=ebuf.at[side], dst_ref=halo.at[1 - side],
            send_sem=edge_send.at[side], recv_sem=edge_recv.at[1 - side],
            device_id={"energy": energy_sides[side][0]}, device_id_type=MESH,
        )

    def slab_copy(side, chunk):
        span = pl.ds(chunk * per, per)
        landing = (left, right)[side]
        source = xv if isinstance(chunk, int) and chunk < raw else own
        return pltpu.make_async_remote_copy(
            src_ref=source.at[:, span], dst_ref=landing.at[:, span],
            send_sem=slab_send.at[side, chunk], recv_sem=slab_recv.at[side, chunk],
            device_id={"atom": sides[side][0]}, device_id_type=MESH,
        )

    def rim_copy(side):
        return pltpu.make_async_remote_copy(
            src_ref=rim, dst_ref=rim_in.at[side],
            send_sem=rim_send.at[side], recv_sem=rim_recv.at[side],
            device_id={"atom": sides[side][0]}, device_id_type=MESH,
        )

    def start_sends(make):
        for side in range(2):

            @pl.when(sides[side][1])
            def _():
                make(side).start()

    def wait_landed(make):
        for side in range(2):

            @pl.when(sides[1 - side][1])
            def _():
                make(side).wait_recv()

    def wait_sent(make):
        for side in range(2):

            @pl.when(sides[side][1])
            def _():
                make(side).wait_send()

    for side in range(2):

        @pl.when(energy_sides[side][1])
        def _():
            edge_copy(side).start()

    for chunk in range(raw):
        start_sends(functools.partial(slab_copy, chunk=chunk))

    def beyond(edge_values):
        return lax.dot_general(edge_values, corner, (((0,), (0,)), ((), ())), preferred_element_type=F32)

    inside = dot(flat[1], band)
    for side in range(2):

        @pl.when(energy_sides[1 - side][1])
        def _():
            edge_copy(side).wait_recv()

    both = halo[0] + halo[1]
    rim[...] = both[:, :split]
    start_sends(rim_copy)
    rest = (inside + beyond(both[:, split:])).astype(BF16)
    own[:, raw_count:] = rest.reshape(2, orb - raw_count, inner, lanes)
    for chunk in range(raw, chunks):
        start_sends(functools.partial(slab_copy, chunk=chunk))
    first_part = (dot(flat[0], band) + beyond(both[:, :split])).astype(BF16)
    own[:, :raw_count] = first_part.reshape(2, raw_count, inner, lanes)

    for copy in loads[4:]:
        copy.wait()
    gf[...] = gv[...].astype(F32)
    ga[...] = jnp.zeros_like(ga)
    for atom in range(atoms):
        picked = [
            gf[pl.ds(atoms * o + atom, bonds, stride=inner), :] for o in range(orb)
        ]
        ga[atom, :, 0:orb] = jnp.concatenate(picked, axis=0).astype(BF16)

    wide = 3 * inner
    source_row, source_col = iota((lanes, wide), 0), iota((lanes, wide), 1)
    spread = jnp.where(source_row == lax.rem(source_col, inner) // atoms, 1.0, 0.0).astype(BF16)
    bond_row, bond_col = iota((bonds, wide), 0), iota((bonds, wide), 1)
    local_id = (bond_col // inner) * atoms + lax.rem(bond_col, atoms)
    for atom in range(atoms):
        near = jnp.zeros((bonds, wide), jnp.int32)
        for bond in range(bonds):
            near = jnp.where(bond_row == bond, nbs[atom, bond], near)
        hit = (near - here_a * atoms + atoms) == local_id
        table = dot(ga[atom], spread).reshape(orb, bonds, wide)
        table = jnp.where(hit[None], table, 0.0).reshape(orb * bonds, wide)
        mbuf[atom * orb * bonds : (atom + 1) * orb * bonds, :] = table.astype(BF16)

    pairs = orb * orb
    span = per * orb * bonds
    lift = jnp.where(
        iota((pairs, orb * bonds), 0) // orb == iota((pairs, orb * bonds), 1) // bonds, 1.0, 0.0
    ).astype(BF16)
    same_bond = lax.rem(iota((orb * bonds, span), 0), bonds) == lax.rem(
        iota((orb * bonds, span), 1), bonds
    )
    same_orbital = lax.rem(iota((pairs, span), 0), orb) == lax.rem(
        iota((pairs, span), 1), orb * bonds
    ) // bonds
    which = iota((lanes, span), 1) // (orb * bonds)

    def build_w(step, carry):
        atom, chunk = step // chunks, lax.rem(step, chunks)
        spread_k = jnp.where(iota((lanes, span), 0) == chunk * per + which, 1.0, 0.0).astype(BF16)
        table = jnp.where(same_bond, dot(ga[atom], spread_k), 0.0).astype(BF16)
        wbuf[atom, chunk] = jnp.where(same_orbital, dot(lift, table), 0.0).astype(BF16)
        return carry

    lax.fori_loop(0, atoms * chunks, build_w, 0)

    tiles = inner // 8
    upper = iota((tiles, 8, lanes), 1) < atoms

    def build_b(o, carry):
        real = xv[0, o].astype(F32).reshape(tiles, 8, lanes)
        imag = xv[1, o].astype(F32).reshape(tiles, 8, lanes)
        for part, value in enumerate((real, imag, real + imag)):
            bf[part, o] = value
            turned = pltpu.roll(value, atoms, 1)
            bdup[part, o, :, 0] = jnp.where(upper, value, turned)
            bdup[part, o, :, 1] = jnp.where(upper, turned, value)
        return carry

    lax.fori_loop(0, orb, build_b, 0)

    for chunk in range(raw):
        wait_landed(functools.partial(slab_copy, chunk=chunk))
    wait_landed(rim_copy)
    for side, landing in enumerate((left, right)):

        @pl.when(sides[1 - side][1])
        def _():
            values = landing[:, :raw_count].reshape(split, lanes)
            sums = (dot(values, band) + beyond(rim_in[side])).astype(BF16)
            landing[:, :raw_count] = sums.reshape(2, raw_count, inner, lanes)

    def chunk_terms(chunk):
        halves = []
        for step in range(per):
            k = chunk * per + step
            stack = jnp.concatenate(
                [
                    jnp.concatenate([left[r, k], own[r, k], right[r, k]], axis=0)
                    for r in range(2)
                ],
                axis=1,
            )
            halves.append(dot(mbuf[...], stack).astype(BF16))
        size = orb * bonds
        return [
            dot(
                wbuf[atom, chunk],
                jnp.concatenate([half[atom * size : (atom + 1) * size] for half in halves], axis=0),
            )
            for atom in range(atoms)
        ]

    for atom, term in enumerate(chunk_terms(0)):
        sacc[atom] = term

    def middle(chunk, carry):
        for atom, term in enumerate(chunk_terms(chunk)):
            sacc[atom] += term
        return carry

    lax.fori_loop(1, raw, middle, 0)

    def landing_chunk(chunk, carry):
        wait_landed(functools.partial(slab_copy, chunk=chunk))
        return middle(chunk, carry)

    lax.fori_loop(raw, chunks - 1, landing_chunk, 0)
    wait_landed(functools.partial(slab_copy, chunk=chunks - 1))
    for atom, term in enumerate(chunk_terms(chunks - 1)):
        total = sacc[atom] + term
        real, imag = total[:, :lanes], total[:, lanes:]
        for part, value in enumerate((real, imag, real + imag)):
            for copy in range(2):
                sdup[part, pl.ds(atom + copy * atoms, pairs, stride=8), :] = value

    def products(factor, other, row):
        sums = [jnp.zeros((tiles, 8, lanes), F32) for _ in range(3)]
        for k in range(orb):
            for part in range(3):
                sums[part] = sums[part] + factor(part, row, k)[None] * other[part, k]
        real = sums[0] - sums[1]
        return real, sums[2] - sums[0] - sums[1]

    def from_sdup(part, row, k):
        return sdup[part, pl.ds(pl.multiple_of((row * orb + k) * 8, 8), 8), :]

    def from_bdup(part, row, k):
        return bdup[part, row, k // 2, k % 2]

    def first(row, carry):
        real, imag = products(from_sdup, bf, row)
        tbuf[0, row] = real
        tbuf[1, row] = imag
        tbuf[2, row] = real + imag
        return carry

    lax.fori_loop(0, orb, first, 0)

    def second(row, carry):
        for part, value in enumerate(products(from_bdup, tbuf, row)):
            total = (value + bf[part, row]).reshape(inner, lanes)
            out_ref[part, row] = total.astype(out_ref.dtype)
        return carry

    lax.fori_loop(0, orb, second, 0)

    for side in range(2):

        @pl.when(energy_sides[side][1])
        def _():
            edge_copy(side).wait_send()

    wait_sent(rim_copy)
    for chunk in range(chunks):
        wait_sent(functools.partial(slab_copy, chunk=chunk))


def per_device(atom_count, energy_count, chunks, raw, bare_green, coupling_grad, neighbours, shifts, strength, occupation):
    _, orb, _, atoms, lanes = bare_green.shape
    bonds = coupling_grad.shape[0]
    inner = orb * atoms
    waves = shifts.shape[0]
    x = bare_green.reshape(2, orb, inner, lanes)
    g = jnp.transpose(coupling_grad, (0, 1, 3, 2)).reshape(bonds * inner, orb)
    per = orb // chunks
    tiles = inner // 8
    any_spec = pl.BlockSpec(memory_space=pl.ANY)
    result = pl.pallas_call(
        functools.partial(kernel, orb, bonds, atoms, atom_count, energy_count, chunks, raw),
        out_shape=jax.ShapeDtypeStruct(x.shape, x.dtype),
        in_specs=[any_spec] * 6,
        out_specs=pl.BlockSpec(memory_space=pltpu.VMEM),
        scratch_shapes=[
            pltpu.VMEM(x.shape, BF16),
            pltpu.VMEM(g.shape, BF16),
            pltpu.SMEM(neighbours.shape, jnp.int32),
            pltpu.VMEM((1, waves), jnp.int32),
            pltpu.VMEM((1, waves), F32),
            pltpu.VMEM((1, waves), F32),
            pltpu.VMEM((2, 8, 2 * orb * inner), BF16),
            pltpu.VMEM((2, 8, 2 * orb * inner), BF16),
            pltpu.VMEM((8, 2 * raw * per * inner), BF16),
            pltpu.VMEM((2, 8, 2 * raw * per * inner), BF16),
            pltpu.VMEM(x.shape, BF16),
            pltpu.VMEM(x.shape, BF16),
            pltpu.VMEM(x.shape, BF16),
            pltpu.VMEM(g.shape, F32),
            pltpu.VMEM((atoms, orb * bonds, lanes), BF16),
            pltpu.VMEM((atoms * orb * bonds, 3 * inner), BF16),
            pltpu.VMEM((atoms, chunks, orb * orb, per * orb * bonds), BF16),
            pltpu.VMEM((3, orb, tiles, 8, lanes), F32),
            pltpu.VMEM((3, orb, tiles, 2, 8, lanes), F32),
            pltpu.VMEM((atoms, orb * orb, 2 * lanes), F32),
            pltpu.VMEM((3, orb * orb * 8, lanes), F32),
            pltpu.VMEM((3, orb, tiles, 8, lanes), F32),
            pltpu.SemaphoreType.DMA((6,)),
            pltpu.SemaphoreType.DMA((2,)),
            pltpu.SemaphoreType.DMA((2,)),
            pltpu.SemaphoreType.DMA((2,)),
            pltpu.SemaphoreType.DMA((2,)),
            pltpu.SemaphoreType.DMA((2, chunks)),
            pltpu.SemaphoreType.DMA((2, chunks)),
        ],
        compiler_params=pltpu.CompilerParams(collective_id=0, has_side_effects=True),
    )(x, g, neighbours, shifts.reshape(1, waves), strength.reshape(1, waves), occupation.reshape(1, waves))
    return result.reshape(bare_green.shape)


def solution(mesh):
    placed = (
        P(None, None, None, "atom", "energy"),
        P(None, None, None, "atom"),
        P("atom", None),
        P(),
        P(),
        P(),
    )
    body = functools.partial(per_device, mesh.shape["atom"], mesh.shape["energy"], 6, 2)
    return jax.shard_map(
        body,
        mesh=mesh,
        in_specs=placed,
        out_specs=P(None, None, None, "atom", "energy"),
        check_vma=False,
    )
```

```python
import functools

import jax
import jax.numpy as jnp
from jax import lax
from jax.experimental import pallas as pl
from jax.experimental.pallas import tpu as pltpu
from jax.sharding import PartitionSpec as P

WIDTH = 4
GROUP = 4
MESH = pl.DeviceIdType.MESH
F32 = jnp.float32
BF16 = jnp.bfloat16


def iota(shape, dim):
    return lax.broadcasted_iota(jnp.int32, shape, dim)


def offset_weight_rows(shifts, strength, occupation):
    row = iota((8, shifts.shape[1]), 0)
    size = jnp.where(row < WIDTH, WIDTH - row, row - (WIDTH - 1))
    extra = jnp.where(row < WIDTH, 0.0, 1.0).astype(F32)
    picked = jnp.where(size == shifts, strength * (occupation + extra), 0.0)
    return jnp.sum(picked, axis=1, keepdims=True).astype(BF16).astype(F32)


def band_from_gap(gap, weights):
    table = jnp.zeros(gap.shape, F32)
    for row in range(8):
        offset = row - WIDTH if row < WIDTH else row - WIDTH + 1
        table = jnp.where(gap == offset, weights[row : row + 1, 0:1], table)
    return table


def dot(left, right):
    return jnp.dot(left, right, preferred_element_type=F32)


def kernel(
    orb, bonds, atoms, atom_count, energy_count, raw,
    x_hbm, g_hbm, nb_hbm, sh_hbm, st_hbm, oc_hbm,
    out_ref,
    xv, gv, nbs, shv, stv, ocv,
    x32, xs, ebuf, halo, rim, rim_in, own, left, right,
    gf, gz, ga, e1, kbuf, bpad, sacc, se, tbuf, out32,
    ready, answer, load_sem, edge_send, edge_recv, rim_send, rim_recv, slab_send, slab_recv,
):
    lanes = xv.shape[-1]
    inner = orb * atoms
    pairs = orb * orb
    high = gz.shape[2]
    here_a = lax.axis_index("atom")
    here_e = lax.axis_index("energy")
    sides = ((here_a + 1, here_a < atom_count - 1), (here_a - 1, here_a > 0))
    energy_sides = ((here_e - 1, here_e > 0), (here_e + 1, here_e < energy_count - 1))

    loads = [
        pltpu.make_async_copy(src, dst, load_sem.at[slot])
        for slot, (src, dst) in enumerate(
            ((x_hbm, xv), (sh_hbm, shv), (st_hbm, stv), (oc_hbm, ocv), (g_hbm, gv), (nb_hbm, nbs))
        )
    ]
    for copy in loads:
        copy.start()
    barrier = pltpu.get_barrier_semaphore()
    expected = jnp.int32(0)
    role = lax.rem(here_a, GROUP)
    heard = (sides[0][1] & (role == GROUP - 1), sides[1][1] & (role != 0))
    answered = (sides[0][1] & (role != GROUP - 1), sides[1][1] & (role == 0))
    for axis, peer, exists in (
        ("atom", sides[0][0], answered[0]),
        ("atom", sides[1][0], answered[1]),
        ("energy", *energy_sides[1]),
        ("energy", energy_sides[0][0], here_e == 1),
    ):

        @pl.when(exists)
        def _():
            pl.semaphore_signal(barrier, inc=1, device_id={axis: peer}, device_id_type=MESH)

    for exists in (heard[0], heard[1], energy_sides[0][1], here_e == 0):
        expected = expected + jnp.where(exists, 1, 0)

    def edge_copy(side):
        return pltpu.make_async_remote_copy(
            src_ref=ebuf.at[side], dst_ref=halo.at[1 - side],
            send_sem=edge_send.at[side], recv_sem=edge_recv.at[1 - side],
            device_id={"energy": energy_sides[side][0]}, device_id_type=MESH,
        )

    def slab_copy(side, slot):
        source = xs if slot < raw else own
        landing = (left, right)[side]
        return pltpu.make_async_remote_copy(
            src_ref=source.at[slot], dst_ref=landing.at[slot],
            send_sem=slab_send.at[side, slot], recv_sem=slab_recv.at[side, slot],
            device_id={"atom": sides[side][0]}, device_id_type=MESH,
        )

    def rim_copy(side):
        return pltpu.make_async_remote_copy(
            src_ref=rim, dst_ref=rim_in.at[side],
            send_sem=rim_send.at[side], recv_sem=rim_recv.at[side],
            device_id={"atom": sides[side][0]}, device_id_type=MESH,
        )

    def start_sends(make):
        for side in range(2):

            @pl.when(heard[side])
            def _():
                make(side).start()

    def wait_landed(make, side):
        @pl.when(sides[1 - side][1])
        def _():
            make(side).wait_recv()

    def wait_sent(make):
        for side in range(2):

            @pl.when(sides[side][1])
            def _():
                make(side).wait_send()

    loads[0].wait()
    x32[...] = xv[...].astype(F32).reshape(2 * orb * inner, lanes)
    for slot in range(atoms):
        for r in range(2):
            rows = x32[pl.ds(r * orb * inner + atoms - 1 - slot, pairs, stride=atoms), :]
            xs[slot, r] = rows.astype(BF16)

    pl.semaphore_wait(barrier, expected)
    for slot in range(raw):
        start_sends(functools.partial(slab_copy, slot=slot))

    for side in range(2):

        @pl.when(heard[side])
        def _():
            pl.semaphore_signal(
                answer.at[1 - side], inc=1, device_id={"atom": sides[side][0]}, device_id_type=MESH
            )

    @pl.when(energy_sides[0][1])
    def _():
        pl.semaphore_signal(ready, inc=1, device_id={"energy": energy_sides[0][0]}, device_id_type=MESH)

    split = raw * 2 * pairs
    offset = -(-split // lanes) * lanes
    ebuf[...] = jnp.zeros_like(ebuf)
    flat = [xs[:raw].reshape(split, lanes), xs[raw:].reshape((atoms - raw) * 2 * pairs, lanes)]
    pick_row, pick_col = iota((16, lanes), 0), iota((16, lanes), 1)
    target = jnp.where(pick_row < 8, pick_row - WIDTH, pick_row - 8 + lanes - WIDTH)
    pick = jnp.where((pick_col == target) & (pick_row >= WIDTH) & (pick_row < 12), 1.0, 0.0).astype(BF16)
    edges = [
        lax.dot_general(pick, part, (((1,), (1,)), ((), ())), preferred_element_type=F32).astype(BF16)
        for part in flat
    ]
    for side in range(2):
        ebuf[side, :, :split] = edges[0][side * 8 : side * 8 + 8]
        ebuf[side, :, offset:] = edges[1][side * 8 : side * 8 + 8]

    for side in range(2):

        @pl.when(energy_sides[side][1])
        def _():
            if side == 1:
                pl.semaphore_wait(ready, 1)
            edge_copy(side).start()

    for side, (_, exists) in enumerate(energy_sides):

        @pl.when(jnp.logical_not(exists))
        def _():
            halo[side] = jnp.zeros(halo.shape[1:], BF16)

    for landing, (_, exists) in ((right, sides[0]), (left, sides[1])):

        @pl.when(jnp.logical_not(exists))
        def _():
            landing[...] = jnp.zeros_like(landing)

    for copy in loads[1:4]:
        copy.wait()
    weights = offset_weight_rows(shv[...], stv[...], ocv[...])
    band = band_from_gap(iota((lanes, lanes), 0) - iota((lanes, lanes), 1), weights).astype(BF16)
    edge_row, edge_col = iota((8, lanes), 0), iota((8, lanes), 1)
    edge_energy = jnp.where(edge_row < WIDTH, edge_row - WIDTH, edge_row - WIDTH + lanes)
    corner = band_from_gap(edge_energy - edge_col, weights).astype(BF16)

    def beyond(edge_values):
        return lax.dot_general(edge_values, corner, (((0,), (0,)), ((), ())), preferred_element_type=F32)

    inside = dot(flat[1], band)
    for side in range(2):

        @pl.when(energy_sides[1 - side][1])
        def _():
            edge_copy(side).wait_recv()

    both = [halo[0, :, :split] + halo[1, :, :split], halo[0, :, offset:] + halo[1, :, offset:]]
    rim[...] = both[0]
    start_sends(rim_copy)
    rest = (inside + beyond(both[1])).astype(BF16)
    own[raw:] = rest.reshape(atoms - raw, 2, pairs, lanes)
    for slot in range(raw, atoms):
        start_sends(functools.partial(slab_copy, slot=slot))
    own[:raw] = (dot(flat[0], band) + beyond(both[0])).astype(BF16).reshape(raw, 2, pairs, lanes)

    for atom in range(atoms):
        for o in range(orb):
            values = [
                x32[pl.ds((r * orb + o) * inner + atom, orb, stride=atoms), :] for r in range(2)
            ]
            for part, value in enumerate((values[0], values[1], values[0] + values[1])):
                bpad[atom, part, o, 0:orb, :] = value

    for copy in loads[4:]:
        copy.wait()
    gf[...] = gv[...].astype(F32)
    gz[...] = jnp.zeros_like(gz)
    for atom in range(atoms):
        for bond in range(bonds):
            gz[atom, bond, 0:orb, 0:orb] = gf[pl.ds(bond * inner + atom, orb, stride=atoms), :]
        ga[atom] = gz[atom].reshape(bonds * high, high).astype(BF16)

    reach = 2 * WIDTH
    others = (reach - 1) * pairs
    last = -(-others // lanes) * lanes
    blocks = kbuf.shape[2] // lanes
    table_row = iota((high, lanes), 0)

    def build(step, carry):
        atom, block = step // blocks, lax.rem(step, blocks)
        column = block * lanes + iota((high, lanes), 1)
        early = column < last
        column = jnp.where(early, column, column - last)
        source = column // pairs
        within = column - source * pairs
        k = within // orb
        source = jnp.where(early, source + 1, 0)
        local_id = atom + source + jnp.where(source >= WIDTH, 1, 0)
        spread_k = jnp.where(table_row == k, 1.0, 0.0).astype(BF16)
        spread_l = jnp.where(table_row == within - k * orb, 1.0, 0.0).astype(BF16)
        first_factor = dot(ga[atom], spread_k).reshape(bonds, high, lanes)
        second_factor = dot(ga[atom], spread_l).reshape(bonds, high, lanes)
        for bond in range(bonds):
            hit = local_id == nbs[atom, bond] - here_a * atoms + atoms
            e1[bond] = jnp.where(hit, first_factor[bond], 0.0)
        for o in range(orb):
            total = jnp.zeros((high, lanes), F32)
            for bond in range(bonds):
                total = total + e1[bond, o : o + 1, :] * second_factor[bond]
            kbuf[atom, o * high : (o + 1) * high, pl.ds(pl.multiple_of(block * lanes, lanes), lanes)] = total.astype(BF16)
        return carry

    lax.fori_loop(0, atoms * blocks, build, 0)

    for side in range(2):

        @pl.when(answered[side])
        def _():
            pl.semaphore_wait(answer.at[side], 1)
            for slot in range(raw):
                slab_copy(side, slot).start()
            rim_copy(side).start()
            for slot in range(raw, atoms):
                slab_copy(side, slot).start()

    def phonon(local_id):
        landing = (left, own, right)[local_id // atoms]
        slot = atoms - 1 - local_id % atoms
        return jnp.concatenate([landing[slot, 0], landing[slot, 1]], axis=1)

    def early_sources(atom):
        ids = [atom + step + (1 if step >= WIDTH else 0) for step in range(1, reach)]
        stack = jnp.concatenate([phonon(each) for each in ids], axis=0)
        sacc[...] = dot(kbuf[atom, :, :others], stack)

    tiles = high // 8
    together = 4

    def products(factor, other, row):
        sums = [[jnp.zeros((high, lanes), F32) for _ in range(3)] for _ in range(together)]
        for k in range(orb):
            for part in range(3):
                value = other(part, k)
                for each in range(together):
                    sums[each][part] = sums[each][part] + factor(part, row + each, k) * value
        return [(total[0] - total[1], total[2] - total[0] - total[1]) for total in sums]

    def finish(atom):
        total = sacc[...] + dot(kbuf[atom, :, last : last + pairs], phonon(atom))
        real, imag = total[:, :lanes], total[:, lanes:]
        for part, value in enumerate((real, imag, real + imag)):
            se[part] = value.reshape(orb, high, lanes)

        def first(step, carry):
            row = step * together
            values = products(
                lambda part, i, k: se[part, i, k : k + 1, :], lambda part, k: bpad[atom, part, k], row
            )
            for each, (real, imag) in enumerate(values):
                tbuf[0, row + each] = real
                tbuf[1, row + each] = imag
                tbuf[2, row + each] = real + imag
            return carry

        lax.fori_loop(0, orb // together, first, 0)

        def second(step, carry):
            row = step * together
            values = products(
                lambda part, i, k: bpad[atom, part, i, k : k + 1, :], lambda part, k: tbuf[part, k], row
            )
            for each, parts in enumerate(values):
                for part, value in enumerate(parts):
                    final = (value + bpad[atom, part, row + each])[:orb]
                    out32[pl.ds((part * orb + row + each) * inner + atom, orb, stride=atoms), :] = final
            return carry

        lax.fori_loop(0, orb // together, second, 0)

    def settle_raw(side):
        landing = (left, right)[side]
        for slot in range(raw):
            wait_landed(functools.partial(slab_copy, slot=slot), side)
        wait_landed(rim_copy, side)

        @pl.when(sides[1 - side][1])
        def _():
            sums = (dot(landing[:raw].reshape(split, lanes), band) + beyond(rim_in[side])).astype(BF16)
            landing[:raw] = sums.reshape(raw, 2, pairs, lanes)

    settle_raw(1)
    for slot in range(raw, atoms):
        wait_landed(functools.partial(slab_copy, slot=slot), 1)
    for atom in range(atoms - 1, -1, -1):
        early_sources(atom)
        slot = atoms - 1 - atom
        if slot == 0:
            settle_raw(0)
        elif slot >= raw:
            wait_landed(functools.partial(slab_copy, slot=slot), 0)
        finish(atom)
    out_ref[...] = out32[...].reshape(out_ref.shape).astype(out_ref.dtype)

    for side in range(2):

        @pl.when(energy_sides[side][1])
        def _():
            edge_copy(side).wait_send()

    wait_sent(rim_copy)
    for slot in range(atoms):
        wait_sent(functools.partial(slab_copy, slot=slot))


def per_device(atom_count, energy_count, bare_green, coupling_grad, neighbours, shifts, strength, occupation):
    _, orb, _, atoms, lanes = bare_green.shape
    bonds = coupling_grad.shape[0]
    inner, pairs = orb * atoms, orb * orb
    waves = shifts.shape[0]
    raw = 1
    high = -(-orb // 16) * 16
    x = bare_green.reshape(2, orb, inner, lanes)
    g = jnp.transpose(coupling_grad, (0, 1, 3, 2)).reshape(bonds * inner, orb)
    columns = sum(-(-count * pairs // lanes) * lanes for count in (2 * WIDTH - 1, 1))
    slab = (atoms, 2, pairs, lanes)
    part = raw * 2 * pairs
    rim_columns = -(-part // lanes) * lanes + (atoms - raw) * 2 * pairs
    any_spec = pl.BlockSpec(memory_space=pl.ANY)
    result = pl.pallas_call(
        functools.partial(kernel, orb, bonds, atoms, atom_count, energy_count, raw),
        out_shape=pltpu.VMEM(x.shape, x.dtype),
        in_specs=[any_spec] * 6,
        out_specs=pl.BlockSpec(memory_space=pltpu.VMEM),
        scratch_shapes=[
            pltpu.VMEM(x.shape, BF16),
            pltpu.VMEM(g.shape, BF16),
            pltpu.SMEM(neighbours.shape, jnp.int32),
            pltpu.VMEM((1, waves), jnp.int32),
            pltpu.VMEM((1, waves), F32),
            pltpu.VMEM((1, waves), F32),
            pltpu.VMEM((2 * orb * inner, lanes), F32),
            pltpu.VMEM(slab, BF16),
            pltpu.VMEM((2, 8, rim_columns), BF16),
            pltpu.VMEM((2, 8, rim_columns), BF16),
            pltpu.VMEM((8, part), BF16),
            pltpu.VMEM((2, 8, part), BF16),
            pltpu.VMEM(slab, BF16),
            pltpu.VMEM(slab, BF16),
            pltpu.VMEM(slab, BF16),
            pltpu.VMEM(g.shape, F32),
            pltpu.VMEM((atoms, bonds, high, high), F32),
            pltpu.VMEM((atoms, bonds * high, high), BF16),
            pltpu.VMEM((bonds, high, lanes), F32),
            pltpu.VMEM((atoms, orb * high, columns), BF16),
            pltpu.VMEM((atoms, 3, orb, high, lanes), F32),
            pltpu.VMEM((orb * high, 2 * lanes), F32),
            pltpu.VMEM((3, orb, high, lanes), F32),
            pltpu.VMEM((3, orb, high, lanes), F32),
            pltpu.VMEM((2 * orb * inner, lanes), F32),
            pltpu.SemaphoreType.REGULAR,
            pltpu.SemaphoreType.REGULAR((2,)),
            pltpu.SemaphoreType.DMA((6,)),
            pltpu.SemaphoreType.DMA((2,)),
            pltpu.SemaphoreType.DMA((2,)),
            pltpu.SemaphoreType.DMA((2,)),
            pltpu.SemaphoreType.DMA((2,)),
            pltpu.SemaphoreType.DMA((2, atoms)),
            pltpu.SemaphoreType.DMA((2, atoms)),
        ],
        compiler_params=pltpu.CompilerParams(collective_id=0, has_side_effects=True),
    )(x, g, neighbours, shifts.reshape(1, waves), strength.reshape(1, waves), occupation.reshape(1, waves))
    return result.reshape(bare_green.shape)


def solution(mesh):
    placed = (
        P(None, None, None, "atom", "energy"),
        P(None, None, None, "atom"),
        P("atom", None),
        P(),
        P(),
        P(),
    )
    body = functools.partial(per_device, mesh.shape["atom"], mesh.shape["energy"])
    return jax.shard_map(
        body,
        mesh=mesh,
        in_specs=placed,
        out_specs=P(None, None, None, "atom", "energy"),
        check_vma=False,
    )
```

```python
import functools

import jax
import jax.numpy as jnp
from jax import lax
from jax.experimental import pallas as pl
from jax.experimental.pallas import tpu as pltpu
from jax.sharding import PartitionSpec as P

WIDTH = 4
GROUP = 4
MESH = pl.DeviceIdType.MESH
F32 = jnp.float32
BF16 = jnp.bfloat16


def iota(shape, dim):
    return lax.broadcasted_iota(jnp.int32, shape, dim)


def offset_weight_rows(shifts, strength, occupation):
    row = iota((8, shifts.shape[1]), 0)
    size = jnp.where(row < WIDTH, WIDTH - row, row - (WIDTH - 1))
    extra = jnp.where(row < WIDTH, 0.0, 1.0).astype(F32)
    picked = jnp.where(size == shifts, strength * (occupation + extra), 0.0)
    return jnp.sum(picked, axis=1, keepdims=True).astype(BF16).astype(F32)


def band_from_gap(gap, weights):
    table = jnp.zeros(gap.shape, F32)
    for row in range(8):
        offset = row - WIDTH if row < WIDTH else row - WIDTH + 1
        table = jnp.where(gap == offset, weights[row : row + 1, 0:1], table)
    return table


def dot(left, right):
    return jnp.dot(left, right, preferred_element_type=F32)


def kernel(
    orb, bonds, atoms, atom_count, energy_count, raw,
    x_hbm, g_hbm, nb_hbm, sh_hbm, st_hbm, oc_hbm,
    out_ref,
    xv, gv, nbs, shv, stv, ocv,
    x32, xs, ebuf, halo, rim, rim_in, own, left, right,
    gf, gz, ga, e1, kbuf, bpad, sacc, se, tbuf, out32,
    ready, answer, load_sem, edge_send, edge_recv, rim_send, rim_recv, slab_send, slab_recv,
):
    lanes = xv.shape[-1]
    inner = orb * atoms
    pairs = orb * orb
    high = gz.shape[2]
    here_a = lax.axis_index("atom")
    here_e = lax.axis_index("energy")
    sides = ((here_a + 1, here_a < atom_count - 1), (here_a - 1, here_a > 0))
    energy_sides = ((here_e - 1, here_e > 0), (here_e + 1, here_e < energy_count - 1))

    loads = [
        pltpu.make_async_copy(src, dst, load_sem.at[slot])
        for slot, (src, dst) in enumerate(
            ((x_hbm, xv), (sh_hbm, shv), (st_hbm, stv), (oc_hbm, ocv), (g_hbm, gv), (nb_hbm, nbs))
        )
    ]
    for copy in loads:
        copy.start()
    barrier = pltpu.get_barrier_semaphore()
    expected = jnp.int32(0)
    role = lax.rem(here_a, GROUP)
    heard = (sides[0][1] & (role == GROUP - 1), sides[1][1] & (role != 0))
    answered = (sides[0][1] & (role != GROUP - 1), sides[1][1] & (role == 0))
    for axis, peer, exists in (
        ("atom", sides[0][0], answered[0]),
        ("atom", sides[1][0], answered[1]),
        ("energy", *energy_sides[1]),
        ("energy", energy_sides[0][0], here_e == 1),
    ):

        @pl.when(exists)
        def _():
            pl.semaphore_signal(barrier, inc=1, device_id={axis: peer}, device_id_type=MESH)

    for exists in (heard[0], heard[1], energy_sides[0][1], here_e == 0):
        expected = expected + jnp.where(exists, 1, 0)

    def edge_copy(side):
        return pltpu.make_async_remote_copy(
            src_ref=ebuf.at[side], dst_ref=halo.at[1 - side],
            send_sem=edge_send.at[side], recv_sem=edge_recv.at[1 - side],
            device_id={"energy": energy_sides[side][0]}, device_id_type=MESH,
        )

    def slab_copy(side, slot):
        source = xs if slot < raw else own
        landing = (left, right)[side]
        return pltpu.make_async_remote_copy(
            src_ref=source.at[slot], dst_ref=landing.at[slot],
            send_sem=slab_send.at[side, slot], recv_sem=slab_recv.at[side, slot],
            device_id={"atom": sides[side][0]}, device_id_type=MESH,
        )

    def rim_copy(side):
        return pltpu.make_async_remote_copy(
            src_ref=rim, dst_ref=rim_in.at[side],
            send_sem=rim_send.at[side], recv_sem=rim_recv.at[side],
            device_id={"atom": sides[side][0]}, device_id_type=MESH,
        )

    def start_sends(make):
        for side in range(2):

            @pl.when(heard[side])
            def _():
                make(side).start()

    def wait_landed(make, side):
        @pl.when(sides[1 - side][1])
        def _():
            make(side).wait_recv()

    def wait_sent(make):
        for side in range(2):

            @pl.when(sides[side][1])
            def _():
                make(side).wait_send()

    loads[0].wait()
    x32[...] = xv[...].astype(F32).reshape(2 * orb * inner, lanes)
    for slot in range(atoms):
        for r in range(2):
            rows = x32[pl.ds(r * orb * inner + atoms - 1 - slot, pairs, stride=atoms), :]
            xs[slot, r] = rows.astype(BF16)

    pl.semaphore_wait(barrier, expected)
    for slot in range(raw):
        start_sends(functools.partial(slab_copy, slot=slot))

    for side in range(2):

        @pl.when(heard[side])
        def _():
            pl.semaphore_signal(
                answer.at[1 - side], inc=1, device_id={"atom": sides[side][0]}, device_id_type=MESH
            )

    @pl.when(energy_sides[0][1])
    def _():
        pl.semaphore_signal(ready, inc=1, device_id={"energy": energy_sides[0][0]}, device_id_type=MESH)

    split = raw * 2 * pairs
    offset = -(-split // lanes) * lanes
    ebuf[...] = jnp.zeros_like(ebuf)
    flat = [xs[:raw].reshape(split, lanes), xs[raw:].reshape((atoms - raw) * 2 * pairs, lanes)]
    pick_row, pick_col = iota((16, lanes), 0), iota((16, lanes), 1)
    target = jnp.where(pick_row < 8, pick_row - WIDTH, pick_row - 8 + lanes - WIDTH)
    pick = jnp.where((pick_col == target) & (pick_row >= WIDTH) & (pick_row < 12), 1.0, 0.0).astype(BF16)
    edges = [
        lax.dot_general(pick, part, (((1,), (1,)), ((), ())), preferred_element_type=F32).astype(BF16)
        for part in flat
    ]
    for side in range(2):
        ebuf[side, :, :split] = edges[0][side * 8 : side * 8 + 8]
        ebuf[side, :, offset:] = edges[1][side * 8 : side * 8 + 8]

    for side in range(2):

        @pl.when(energy_sides[side][1])
        def _():
            if side == 1:
                pl.semaphore_wait(ready, 1)
            edge_copy(side).start()

    for side, (_, exists) in enumerate(energy_sides):

        @pl.when(jnp.logical_not(exists))
        def _():
            halo[side] = jnp.zeros(halo.shape[1:], BF16)

    for landing, (_, exists) in ((right, sides[0]), (left, sides[1])):

        @pl.when(jnp.logical_not(exists))
        def _():
            landing[...] = jnp.zeros_like(landing)

    for copy in loads[1:4]:
        copy.wait()
    weights = offset_weight_rows(shv[...], stv[...], ocv[...])
    band = band_from_gap(iota((lanes, lanes), 0) - iota((lanes, lanes), 1), weights).astype(BF16)
    edge_row, edge_col = iota((8, lanes), 0), iota((8, lanes), 1)
    edge_energy = jnp.where(edge_row < WIDTH, edge_row - WIDTH, edge_row - WIDTH + lanes)
    corner = band_from_gap(edge_energy - edge_col, weights).astype(BF16)

    def beyond(edge_values):
        return lax.dot_general(edge_values, corner, (((0,), (0,)), ((), ())), preferred_element_type=F32)

    inside = dot(flat[1], band)
    for side in range(2):

        @pl.when(energy_sides[1 - side][1])
        def _():
            edge_copy(side).wait_recv()

    both = [halo[0, :, :split] + halo[1, :, :split], halo[0, :, offset:] + halo[1, :, offset:]]
    rim[...] = both[0]
    start_sends(rim_copy)
    rest = (inside + beyond(both[1])).astype(BF16)
    own[raw:] = rest.reshape(atoms - raw, 2, pairs, lanes)
    for order in zip(range(raw, atoms), reversed(range(raw, atoms))):
        for side in range(2):

            @pl.when(heard[side])
            def _():
                slab_copy(side, order[side]).start()

    own[:raw] = (dot(flat[0], band) + beyond(both[0])).astype(BF16).reshape(raw, 2, pairs, lanes)

    for atom in range(atoms):
        for o in range(orb):
            values = [
                x32[pl.ds((r * orb + o) * inner + atom, orb, stride=atoms), :] for r in range(2)
            ]
            for part, value in enumerate((values[0], values[1], values[0] + values[1])):
                bpad[atom, part, o, 0:orb, :] = value

    for copy in loads[4:]:
        copy.wait()
    gf[...] = gv[...].astype(F32)
    gz[...] = jnp.zeros_like(gz)
    for atom in range(atoms):
        for bond in range(bonds):
            gz[atom, bond, 0:orb, 0:orb] = gf[pl.ds(bond * inner + atom, orb, stride=atoms), :]
        ga[atom] = gz[atom].reshape(bonds * high, high).astype(BF16)

    reach = 2 * WIDTH
    others = (reach - 1) * pairs
    last = -(-others // lanes) * lanes
    blocks = kbuf.shape[2] // lanes
    table_row = iota((high, lanes), 0)

    def build(step, carry):
        atom, block = step // blocks, lax.rem(step, blocks)
        column = block * lanes + iota((high, lanes), 1)
        early = column < last
        column = jnp.where(early, column, column - last)
        source = column // pairs
        within = column - source * pairs
        k = within // orb
        source = jnp.where(early, source + 1, 0)
        local_id = atom + source + jnp.where(source >= WIDTH, 1, 0)
        spread_k = jnp.where(table_row == k, 1.0, 0.0).astype(BF16)
        spread_l = jnp.where(table_row == within - k * orb, 1.0, 0.0).astype(BF16)
        first_factor = dot(ga[atom], spread_k).reshape(bonds, high, lanes)
        second_factor = dot(ga[atom], spread_l).reshape(bonds, high, lanes)
        for bond in range(bonds):
            hit = local_id == nbs[atom, bond] - here_a * atoms + atoms
            e1[bond] = jnp.where(hit, first_factor[bond], 0.0)
        for o in range(orb):
            total = jnp.zeros((high, lanes), F32)
            for bond in range(bonds):
                total = total + e1[bond, o : o + 1, :] * second_factor[bond]
            kbuf[atom, o * high : (o + 1) * high, pl.ds(pl.multiple_of(block * lanes, lanes), lanes)] = total.astype(BF16)
        return carry

    lax.fori_loop(0, atoms * blocks, build, 0)

    for side in range(2):

        @pl.when(answered[side])
        def _():
            pl.semaphore_wait(answer.at[side], 1)
            for slot in range(raw):
                slab_copy(side, slot).start()
            rim_copy(side).start()
            for slot in range(raw, atoms) if side == 0 else reversed(range(raw, atoms)):
                slab_copy(side, slot).start()

    def phonon(local_id):
        landing = (left, own, right)[local_id // atoms]
        slot = atoms - 1 - local_id % atoms
        return jnp.concatenate([landing[slot, 0], landing[slot, 1]], axis=1)

    def early_sources(atom):
        ids = [atom + step + (1 if step >= WIDTH else 0) for step in range(1, reach)]
        stack = jnp.concatenate([phonon(each) for each in ids], axis=0)
        sacc[...] = dot(kbuf[atom, :, :others], stack)

    tiles = high // 8
    together = 4

    def products(factor, other, row):
        sums = [[jnp.zeros((high, lanes), F32) for _ in range(3)] for _ in range(together)]
        for k in range(orb):
            for part in range(3):
                value = other(part, k)
                for each in range(together):
                    sums[each][part] = sums[each][part] + factor(part, row + each, k) * value
        return [(total[0] - total[1], total[2] - total[0] - total[1]) for total in sums]

    def finish(atom):
        total = sacc[...] + dot(kbuf[atom, :, last : last + pairs], phonon(atom))
        real, imag = total[:, :lanes], total[:, lanes:]
        for part, value in enumerate((real, imag, real + imag)):
            se[part] = value.reshape(orb, high, lanes)

        def first(step, carry):
            row = step * together
            values = products(
                lambda part, i, k: se[part, i, k : k + 1, :], lambda part, k: bpad[atom, part, k], row
            )
            for each, (real, imag) in enumerate(values):
                tbuf[0, row + each] = real
                tbuf[1, row + each] = imag
                tbuf[2, row + each] = real + imag
            return carry

        lax.fori_loop(0, orb // together, first, 0)

        def second(step, carry):
            row = step * together
            values = products(
                lambda part, i, k: bpad[atom, part, i, k : k + 1, :], lambda part, k: tbuf[part, k], row
            )
            for each, parts in enumerate(values):
                for part, value in enumerate(parts):
                    final = (value + bpad[atom, part, row + each])[:orb]
                    out32[pl.ds((part * orb + row + each) * inner + atom, orb, stride=atoms), :] = final
            return carry

        lax.fori_loop(0, orb // together, second, 0)

    def settle_raw(side):
        landing = (left, right)[side]
        for slot in range(raw):
            wait_landed(functools.partial(slab_copy, slot=slot), side)
        wait_landed(rim_copy, side)

        @pl.when(sides[1 - side][1])
        def _():
            sums = (dot(landing[:raw].reshape(split, lanes), band) + beyond(rim_in[side])).astype(BF16)
            landing[:raw] = sums.reshape(raw, 2, pairs, lanes)

    settle_raw(1)

    @pl.when(here_a == 0)
    def _():
        for atom in range(atoms):
            slot = atoms - 1 - atom
            if slot >= raw:
                wait_landed(functools.partial(slab_copy, slot=slot), 1)
            early_sources(atom)
            finish(atom)

    @pl.when(here_a > 0)
    def _():
        for slot in reversed(range(raw, atoms)):
            wait_landed(functools.partial(slab_copy, slot=slot), 1)
        for atom in range(atoms - 1, -1, -1):
            early_sources(atom)
            slot = atoms - 1 - atom
            if slot == 0:
                settle_raw(0)
            elif slot >= raw:
                wait_landed(functools.partial(slab_copy, slot=slot), 0)
            finish(atom)

    out_ref[...] = out32[...].reshape(out_ref.shape).astype(out_ref.dtype)

    for side in range(2):

        @pl.when(energy_sides[side][1])
        def _():
            edge_copy(side).wait_send()

    wait_sent(rim_copy)
    for slot in range(atoms):
        wait_sent(functools.partial(slab_copy, slot=slot))


def per_device(atom_count, energy_count, bare_green, coupling_grad, neighbours, shifts, strength, occupation):
    _, orb, _, atoms, lanes = bare_green.shape
    bonds = coupling_grad.shape[0]
    inner, pairs = orb * atoms, orb * orb
    waves = shifts.shape[0]
    raw = 1
    high = -(-orb // 16) * 16
    x = bare_green.reshape(2, orb, inner, lanes)
    g = jnp.transpose(coupling_grad, (0, 1, 3, 2)).reshape(bonds * inner, orb)
    columns = sum(-(-count * pairs // lanes) * lanes for count in (2 * WIDTH - 1, 1))
    slab = (atoms, 2, pairs, lanes)
    part = raw * 2 * pairs
    rim_columns = -(-part // lanes) * lanes + (atoms - raw) * 2 * pairs
    any_spec = pl.BlockSpec(memory_space=pl.ANY)
    result = pl.pallas_call(
        functools.partial(kernel, orb, bonds, atoms, atom_count, energy_count, raw),
        out_shape=pltpu.VMEM(x.shape, x.dtype),
        in_specs=[any_spec] * 6,
        out_specs=pl.BlockSpec(memory_space=pltpu.VMEM),
        scratch_shapes=[
            pltpu.VMEM(x.shape, BF16),
            pltpu.VMEM(g.shape, BF16),
            pltpu.SMEM(neighbours.shape, jnp.int32),
            pltpu.VMEM((1, waves), jnp.int32),
            pltpu.VMEM((1, waves), F32),
            pltpu.VMEM((1, waves), F32),
            pltpu.VMEM((2 * orb * inner, lanes), F32),
            pltpu.VMEM(slab, BF16),
            pltpu.VMEM((2, 8, rim_columns), BF16),
            pltpu.VMEM((2, 8, rim_columns), BF16),
            pltpu.VMEM((8, part), BF16),
            pltpu.VMEM((2, 8, part), BF16),
            pltpu.VMEM(slab, BF16),
            pltpu.VMEM(slab, BF16),
            pltpu.VMEM(slab, BF16),
            pltpu.VMEM(g.shape, F32),
            pltpu.VMEM((atoms, bonds, high, high), F32),
            pltpu.VMEM((atoms, bonds * high, high), BF16),
            pltpu.VMEM((bonds, high, lanes), F32),
            pltpu.VMEM((atoms, orb * high, columns), BF16),
            pltpu.VMEM((atoms, 3, orb, high, lanes), F32),
            pltpu.VMEM((orb * high, 2 * lanes), F32),
            pltpu.VMEM((3, orb, high, lanes), F32),
            pltpu.VMEM((3, orb, high, lanes), F32),
            pltpu.VMEM((2 * orb * inner, lanes), F32),
            pltpu.SemaphoreType.REGULAR,
            pltpu.SemaphoreType.REGULAR((2,)),
            pltpu.SemaphoreType.DMA((6,)),
            pltpu.SemaphoreType.DMA((2,)),
            pltpu.SemaphoreType.DMA((2,)),
            pltpu.SemaphoreType.DMA((2,)),
            pltpu.SemaphoreType.DMA((2,)),
            pltpu.SemaphoreType.DMA((2, atoms)),
            pltpu.SemaphoreType.DMA((2, atoms)),
        ],
        compiler_params=pltpu.CompilerParams(collective_id=0, has_side_effects=True),
    )(x, g, neighbours, shifts.reshape(1, waves), strength.reshape(1, waves), occupation.reshape(1, waves))
    return result.reshape(bare_green.shape)


def solution(mesh):
    placed = (
        P(None, None, None, "atom", "energy"),
        P(None, None, None, "atom"),
        P("atom", None),
        P(),
        P(),
        P(),
    )
    body = functools.partial(per_device, mesh.shape["atom"], mesh.shape["energy"])
    return jax.shard_map(
        body,
        mesh=mesh,
        in_specs=placed,
        out_specs=P(None, None, None, "atom", "energy"),
        check_vma=False,
    )
```
